32 devices in a mesh: axial: 8 (over y, x, core), azim: 4 (over z).
Axes of the slice: x: 2, y: 2, z: 4, core: 2. Of those that a mesh axis runs over, the one named last changes fastest.
Arguments:
- state: float32 [5, 16, 1024, 96], P(None, 'axial', 'azim'), as said below
- start: float32 [5, 16, 1024, 96], P(None, 'axial', 'azim'), as said below
- modes: int32 [64], replicated, may hold values from 1 to 512, as said below
Outputs:
- section: float32 [5, 16, 1024, 96], P(None, 'axial', 'azim')
The draws below stay inside these ranges and needn't reach their ends.
Inputs may be any that keep to these rules, and one draw needn't show every extreme that they name: Cycle j keeps the modes 0 to modes[j] - 1; modes[j] lies between 8 * (j + 1) and 2 * 8 * (j + 1), capped at 512, which the last cycle reaches. `state`: the density (field 0) lies between 0.85 and 1.15. `start`: the density (field 0) lies between 0.85 and 1.15.
All inputs are finite; a program needn't handle non-finite values.
Results may differ from the reference program's by a relative error of at most 0.00005.
Values sent between devices are 32-bit elements; how exact they have to be, the bound alone decides.
A program may use at most 64 MiB of HBM per device.

```python
import math
import jax
import jax.numpy as jnp
from jax import lax

NTH = 1024
NR = 96
NIN = 64
X_DEV = 2
NA = 16
MSTEP = 8
N_AXIAL = 8


GAMMA = 1.4


def make_state(key):
    keys = jax.random.split(key, 5)
    shape = (NA, NTH, NR)
    density = 1.0 + jax.random.uniform(keys[0], shape, jnp.float32, -0.15, 0.15)
    axial_speed = 1.5 + 0.3 * jnp.clip(jax.random.normal(keys[1], shape, jnp.float32), -4.0, 4.0)
    radial_speed = 0.3 * jnp.clip(jax.random.normal(keys[2], shape, jnp.float32), -4.0, 4.0)
    swirl_speed = 0.3 * jnp.clip(jax.random.normal(keys[3], shape, jnp.float32), -4.0, 4.0)
    pressure = jax.random.uniform(keys[4], shape, jnp.float32, 0.6, 0.85)
    kinetic = axial_speed * axial_speed + radial_speed * radial_speed + swirl_speed * swirl_speed
    energy = pressure / (GAMMA - 1.0) + 0.5 * density * kinetic
    fields = jnp.stack([density, density * axial_speed, density * radial_speed, density * swirl_speed, energy])
    return fields.astype(jnp.float32)


def draw_state(key, part):
    return make_state(jax.random.fold_in(key, 11))


def draw_start(key, part):
    return make_state(jax.random.fold_in(key, 23))


def draw_modes(key, part):
    own_key = jax.random.fold_in(key, 37)
    lower = MSTEP * (jnp.arange(NIN, dtype=jnp.int32) + 1)
    extra = jax.random.randint(own_key, (NIN,), 0, lower + 1, dtype=jnp.int32)
    return jnp.minimum(lower + extra, NTH // 2).astype(jnp.int32)


def setup_inputs(seed: int = 0) -> dict:
    arg_keys = jax.random.split(jax.random.key(seed), 4)
    return {
        "state": draw_state(jax.random.fold_in(arg_keys[3], 71), 0),
        "start": draw_start(jax.random.fold_in(arg_keys[3], 71), 0),
        "modes": draw_modes(jax.random.fold_in(arg_keys[3], 71), 0),
    }


GAMMA = 1.4
STEP_DT = 0.05


def central_diff(values, dimension):
    length = values.shape[dimension] - 4

    def part_at(offset):
        return lax.slice_in_dim(values, offset, offset + length, axis=dimension)

    return (8.0 * (part_at(3) - part_at(1)) - (part_at(4) - part_at(0))) / 12.0


def pressure_of(values, inverse):
    kinetic = (values[1] * values[1] + values[2] * values[2] + values[3] * values[3]) * inverse
    return (GAMMA - 1.0) * (values[4] - 0.5 * kinetic)


def flux_along(values, direction):
    inverse = 1.0 / values[0]
    velocity = values[direction] * inverse
    pressure = pressure_of(values, inverse)
    components = [values[direction], values[1] * velocity, values[2] * velocity, values[3] * velocity, (values[4] + pressure) * velocity]
    components[direction] = components[direction] + pressure
    return jnp.stack(components)


def rates_of(padded, dtheta):
    axial_cells = padded[:, :, 2:-2, 2:-2]
    azimuth_cells = padded[:, 2:-2, :, 2:-2]
    radial_cells = padded[:, 2:-2, 2:-2, :]
    centre = padded[:, 2:-2, 2:-2, 2:-2]
    radius_all = jnp.arange(padded.shape[3], dtype=jnp.float32) - 1.5
    inv_radius = 1.0 / radius_all[2:-2]
    axial_term = central_diff(flux_along(axial_cells, 1), 1)
    radial_term = central_diff(flux_along(radial_cells, 2) * radius_all, 3) * inv_radius
    azimuth_term = central_diff(flux_along(azimuth_cells, 3), 2) * (inv_radius / dtheta)
    inverse = 1.0 / centre[0]
    pressure = pressure_of(centre, inverse)
    source_radial = (centre[3] * centre[3] * inverse + pressure) * inv_radius
    source_azimuth = -(centre[2] * centre[3] * inverse) * inv_radius
    totals = -(axial_term + radial_term + azimuth_term)
    return jnp.stack([totals[0], totals[1], totals[2] + source_radial, totals[3] + source_azimuth, totals[4]])


def radial_extend(haloed, partner):
    signs = jnp.array([1.0, 1.0, -1.0, -1.0, 1.0], dtype=jnp.float32).reshape(5, 1, 1, 1)
    ghost = jnp.flip(partner, 3) * signs
    rim_axial = (haloed.shape[1] - ghost.shape[1]) // 2
    rim_theta = (haloed.shape[2] - ghost.shape[2]) // 2
    ghost = jnp.pad(ghost, ((0, 0), (rim_axial, rim_axial), (rim_theta, rim_theta), (0, 0)))
    outer_cycles = jnp.repeat(haloed[..., -1:], 2, axis=3)
    return jnp.concatenate([ghost.astype(haloed.dtype), haloed, outer_cycles], axis=3)


def reference(state, start, modes):
    half_modes = NTH // 2
    inner = state[..., :NIN]
    spectrum = jnp.fft.rfft(inner, axis=2)
    wavenumbers = jnp.arange(half_modes + 1, dtype=jnp.int32)
    keep_mask = wavenumbers[:, None] < modes[None, :]
    spectrum = jnp.where(keep_mask, spectrum, jnp.zeros_like(spectrum))
    smooth_inner = jnp.fft.irfft(spectrum, n=NTH, axis=2).astype(state.dtype)
    smoothed = jnp.concatenate([smooth_inner, state[..., NIN:]], axis=3)
    partner = jnp.roll(smoothed[..., :2], half_modes, axis=2)
    extended = radial_extend(smoothed, partner)
    extended = jnp.concatenate([extended[:, :, -2:], extended, extended[:, :, :2]], axis=2)
    extended = jnp.concatenate([extended[:, -2:], extended, extended[:, :2]], axis=1)
    dtheta = 2.0 * math.pi / NTH

    def one_slab(slab_index):
        piece = lax.dynamic_slice_in_dim(extended, slab_index * X_DEV, X_DEV + 4, axis=1)
        return rates_of(piece, dtheta)

    slab_rates = lax.map(one_slab, jnp.arange(N_AXIAL, dtype=jnp.int32))
    rate = jnp.moveaxis(slab_rates, 0, 1).reshape(state.shape)
    return start + STEP_DT * rate
```

```python
import math

import jax
import jax.numpy as jnp
import numpy as np
from jax import lax
from jax.sharding import PartitionSpec as P

NTH = 1024
NIN = 64


GAMMA = 1.4
STEP_DT = 0.05


def swapped(value, axis, bit):
    return lax.ppermute(value, axis, [(i, i ^ 1 << bit) for i in range(lax.axis_size(axis))])


def with_halo(cells, sides, width):
    for axis, dim in sides:
        count = lax.axis_size(axis)
        head = lax.slice_in_dim(cells, 0, width, axis=dim)
        tail = lax.slice_in_dim(cells, cells.shape[dim] - width, cells.shape[dim], axis=dim)
        cells = jnp.concatenate(
            [
                lax.ppermute(tail, axis, [(i, (i + 1) % count) for i in range(count)]),
                cells,
                lax.ppermute(head, axis, [((i + 1) % count, i) for i in range(count)]),
            ],
            axis=dim,
        )
    return cells


def central_diff(values, dimension):
    length = values.shape[dimension] - 4

    def part_at(offset):
        return lax.slice_in_dim(values, offset, offset + length, axis=dimension)

    return (8.0 * (part_at(3) - part_at(1)) - (part_at(4) - part_at(0))) / 12.0


def pressure_of(values, inverse):
    kinetic = (values[1] * values[1] + values[2] * values[2] + values[3] * values[3]) * inverse
    return (GAMMA - 1.0) * (values[4] - 0.5 * kinetic)


def flux_along(values, direction):
    inverse = 1.0 / values[0]
    velocity = values[direction] * inverse
    pressure = pressure_of(values, inverse)
    components = [
        values[direction],
        values[1] * velocity,
        values[2] * velocity,
        values[3] * velocity,
        (values[4] + pressure) * velocity,
    ]
    components[direction] = components[direction] + pressure
    return jnp.stack(components)


def rates_of(padded, dtheta):
    axial_cells = padded[:, :, 2:-2, 2:-2]
    azimuth_cells = padded[:, 2:-2, :, 2:-2]
    radial_cells = padded[:, 2:-2, 2:-2, :]
    centre = padded[:, 2:-2, 2:-2, 2:-2]
    radius_all = jnp.arange(padded.shape[3], dtype=jnp.float32) - 1.5
    inv_radius = 1.0 / radius_all[2:-2]
    axial_term = central_diff(flux_along(axial_cells, 1), 1)
    radial_term = central_diff(flux_along(radial_cells, 2) * radius_all, 3) * inv_radius
    azimuth_term = central_diff(flux_along(azimuth_cells, 3), 2) * (inv_radius / dtheta)
    inverse = 1.0 / centre[0]
    pressure = pressure_of(centre, inverse)
    source_radial = (centre[3] * centre[3] * inverse + pressure) * inv_radius
    source_azimuth = -(centre[2] * centre[3] * inverse) * inv_radius
    totals = -(axial_term + radial_term + azimuth_term)
    return jnp.stack(
        [totals[0], totals[1], totals[2] + source_radial, totals[3] + source_azimuth, totals[4]]
    )


def radial_extend(haloed, partner):
    signs = jnp.array([1.0, 1.0, -1.0, -1.0, 1.0], dtype=jnp.float32).reshape(5, 1, 1, 1)
    ghost = jnp.flip(partner, 3) * signs
    rim_axial = (haloed.shape[1] - ghost.shape[1]) // 2
    rim_theta = (haloed.shape[2] - ghost.shape[2]) // 2
    ghost = jnp.pad(ghost, ((0, 0), (rim_axial, rim_axial), (rim_theta, rim_theta), (0, 0)))
    outer_cycles = jnp.repeat(haloed[..., -1:], 2, axis=3)
    return jnp.concatenate([ghost, haloed, outer_cycles], axis=3)


def fourier_basis():
    half_modes = NTH // 2
    block = 32
    waves = np.arange(half_modes)
    coarse = np.exp(2j * np.pi * (np.arange(0, NTH, block)[:, None] * waves % NTH) / NTH)
    fine = np.exp(2j * np.pi * (np.arange(block)[:, None] * waves % NTH) / NTH)
    coarse_cos = jnp.asarray(coarse.real, jnp.float32)[:, None]
    coarse_sin = jnp.asarray(coarse.imag, jnp.float32)[:, None]
    fine_cos = jnp.asarray(fine.real, jnp.float32)[None]
    fine_sin = jnp.asarray(fine.imag, jnp.float32)[None]
    cosines = (coarse_cos * fine_cos - coarse_sin * fine_sin).reshape(NTH, half_modes)
    sines = (coarse_sin * fine_cos + coarse_cos * fine_sin).reshape(NTH, half_modes)
    return jnp.concatenate([cosines, sines], axis=1)


def truncate_cycles(slab, local_modes):
    items, cycles, cells = slab.shape
    half_modes = NTH // 2
    basis = fourier_basis()
    rows = slab.reshape(items * cycles, cells)
    coeffs = jnp.dot(rows, basis, precision=lax.Precision.HIGH)
    wave = jnp.arange(2 * half_modes, dtype=jnp.int32) % half_modes
    weight = jnp.where(wave == 0, 1.0 / NTH, 2.0 / NTH).astype(jnp.float32)
    kept = jnp.where(wave[None, :] < local_modes[:, None], weight[None, :], 0.0)
    coeffs = (coeffs.reshape(items, cycles, 2 * half_modes) * kept[None]).reshape(items * cycles, -1)
    series = lax.dot_general(
        coeffs, basis, (((1,), (1,)), ((), ())), precision=lax.Precision.HIGH
    )
    return series.reshape(items, cycles, cells)


def shards(state, start, modes):
    field_count, axial_local, theta_local, cycle_total = state.shape
    azim_size = lax.axis_size("azim")
    azim_index = lax.axis_index("azim")
    cycles_local = NIN // azim_size
    item_count = field_count * axial_local
    inner = state[..., :NIN].transpose(0, 1, 3, 2).reshape(item_count, NIN, theta_local)
    local_modes = lax.dynamic_slice_in_dim(modes, azim_index * cycles_local, cycles_local)
    smoothed = truncate_cycles(
        lax.all_to_all(inner, "azim", split_axis=1, concat_axis=2, tiled=True),
        local_modes,
    )
    exchanged = lax.all_to_all(smoothed, "azim", split_axis=2, concat_axis=1, tiled=True)
    smooth_inner = exchanged.reshape(field_count, axial_local, NIN, theta_local).transpose(
        0, 1, 3, 2
    )
    smoothed_state = jnp.concatenate([smooth_inner, state[..., NIN:]], axis=3)
    partner = swapped(smoothed_state[..., :2], "azim", azim_size.bit_length() - 2)
    haloed = with_halo(smoothed_state, (("axial", 1), ("azim", 2)), 2)
    padded = radial_extend(haloed, partner)
    rate = rates_of(padded, 2.0 * math.pi / NTH)
    return start + STEP_DT * rate


def solution(mesh):
    in_specs = (P(None, "axial", "azim", None), P(None, "axial", "azim", None), P())
    out_specs = P(None, "axial", "azim", None)
    return jax.shard_map(shards, mesh=mesh, in_specs=in_specs, out_specs=out_specs, check_vma=False)
```

```python
import functools
import math

import jax
import jax.numpy as jnp
import numpy as np
from jax import lax
from jax.experimental import pallas as pl
from jax.experimental.pallas import tpu as pltpu
from jax.sharding import PartitionSpec as P

NTH = 1024
NIN = 64
MSTEP = 8
STEP_DT = 0.05
LANES = 128
RIM = 8
F32 = jnp.float32
BF16 = jnp.bfloat16
MESH = pl.DeviceIdType.MESH


def split_np(values):
    high = values.astype(np.float32).astype(jnp.bfloat16)
    low = (values - high.astype(np.float64)).astype(np.float32).astype(jnp.bfloat16)
    return np.stack([high, low])


@functools.lru_cache(None)
def plan(cells):
    order = np.arange(1, NIN + 1)
    kept = np.minimum(2 * MSTEP * order, NTH // 2)
    dropped = NTH // 2 + 1 - np.minimum(MSTEP * order, NTH // 2)
    use_kept = kept <= dropped
    bound = np.where(use_kept, kept, dropped)
    first_dropped = int(np.argmin(use_kept))
    ranked = np.argsort(-bound, kind="stable")
    pairs = NIN // 2
    top, bottom = ranked[:pairs], ranked[::-1][:pairs]
    rows = int(-(-np.max(bound[top] + bound[bottom]) // 16) * 16)
    wave = np.arange(rows)
    angle = lambda n, q: 2 * np.pi * ((n * q) % NTH) / NTH
    forward = []
    for waves in (wave, wave[::-1]):
        phase = angle(np.arange(cells)[None, :], waves[:, None])
        forward.append(split_np(np.concatenate([np.cos(phase), np.sin(phase)], 0)))
    inverse = []
    for waves in (wave, wave[::-1]):
        phase = angle(np.arange(-RIM, cells + RIM)[:, None], waves[None, :])
        inverse.append(split_np(np.concatenate([np.cos(phase), np.sin(phase)], 1)))
    slots = LANES // pairs
    place = np.zeros((slots + slots // 2, LANES, 2 * LANES), np.float32)
    ghost = np.zeros((slots + slots // 2, LANES, LANES), np.float32)
    for slot in range(slots):
        for pair in range(pairs):
            place[slot, top[pair], slot * pairs + pair] = 1
            place[slot, bottom[pair], LANES + slot * pairs + pair] = 1
            if bottom[pair] < 2:
                ghost[slot, slot * pairs + pair, LANES - 1 - bottom[pair]] = 1
    half = slots // 2
    for k in range(half):
        place[slots + k] = place[k] + place[half + k]
        ghost[slots + k] = ghost[k] + ghost[half + k]
    top_rows = np.tile(bound[top], slots)
    wave_of = np.where(wave[:, None] < top_rows[None, :], wave[:, None], rows - 1 - wave[:, None])
    turn = angle(cells, wave_of)
    return dict(
        rows=rows,
        top=top,
        bottom=bottom,
        slots=slots,
        first_dropped=first_dropped,
        top_rows=top_rows.astype(np.int32),
        forward=np.stack(forward),
        inverse=np.stack(inverse),
        place=place.astype(jnp.bfloat16),
        back=place.transpose(0, 2, 1).astype(jnp.bfloat16),
        ghost=ghost.astype(jnp.bfloat16),
        turn=np.stack([np.cos(turn), np.sin(turn)]).astype(np.float32),
    )


def split(values):
    high = values.astype(BF16)
    return high, (values - high.astype(F32)).astype(BF16)


def mm(a, b):
    return jnp.dot(a, b, preferred_element_type=F32)


def fluxes(values, direction):
    inverse = 1.0 / values[0]
    velocity = values[direction] * inverse
    kinetic = (values[1] * values[1] + values[2] * values[2] + values[3] * values[3]) * inverse
    pressure = 0.4 * (values[4] - 0.5 * kinetic)
    parts = [
        values[direction],
        values[1] * velocity,
        values[2] * velocity,
        values[3] * velocity,
        (values[4] + pressure) * velocity,
    ]
    parts[direction] = parts[direction] + pressure
    return parts, inverse, pressure


def kernel(
    cfg,
    state, limits, forward, inverse, place, back, ghost, turn,
    out,
    ext, outer_own, outer_left, outer_right, inner_own, inner_left, inner_right,
    own, to_right, to_left, from_left, from_right, spectrum,
    halo_send, halo_recv, outer_send, outer_recv, inner_send, inner_recv, wave_send, wave_recv,
):
    rows, first_dropped = cfg["rows"], cfg["first_dropped"]
    half = rows // 2
    fields, cells, cycles = state.shape[0], state.shape[2], out.shape[3]
    tall = cells + 2 * RIM
    d, count = lax.axis_index("azim"), lax.axis_size("azim")
    a, ring = lax.axis_index("axial"), lax.axis_size("axial")
    z_right = {"azim": lax.rem(d + 1, count)}
    z_left = {"azim": lax.rem(d + count - 1, count)}
    x_right = {"axial": lax.rem(a + 1, ring)}
    x_left = {"axial": lax.rem(a + ring - 1, ring)}

    def remote(src, dst, send, recv, device):
        return pltpu.make_async_remote_copy(
            src_ref=src, dst_ref=dst, send_sem=send, recv_sem=recv,
            device_id=device, device_id_type=MESH,
        )

    barrier = pltpu.get_barrier_semaphore()
    for device in (z_right, z_left, x_right, x_left):
        pl.semaphore_signal(barrier, inc=1, device_id=device, device_id_type=MESH)
    pl.semaphore_wait(barrier, 4)

    halos = [
        remote(
            state.at[:, :, pl.ds(cells - RIM, RIM)], ext.at[:, :, pl.ds(0, RIM)],
            halo_send.at[0], halo_recv.at[0], z_right,
        ),
        remote(
            state.at[:, :, pl.ds(0, RIM)], ext.at[:, :, pl.ds(cells + RIM, RIM)],
            halo_send.at[1], halo_recv.at[1], z_left,
        ),
    ]
    outers = [
        remote(outer_own, outer_left, outer_send.at[0], outer_recv.at[0], x_right),
        remote(outer_own, outer_right, outer_send.at[1], outer_recv.at[1], x_left),
    ]
    chunks = 5
    rights = [
        remote(to_right.at[c], from_left.at[c], wave_send.at[0, c], wave_recv.at[0, c], z_right)
        for c in range(chunks)
    ]
    lefts = [
        remote(to_left.at[c], from_right.at[c], wave_send.at[1, c], wave_recv.at[1, c], z_left)
        for c in range(chunks)
    ]
    inners = [
        [
            remote(inner_own.at[f], inner_left.at[f], inner_send.at[0, f], inner_recv.at[0, f], x_right),
            remote(inner_own.at[f], inner_right.at[f], inner_send.at[1, f], inner_recv.at[1, f], x_left),
        ]
        for f in range(fields)
    ]
    is_first, is_last = d == 0, d == count - 1

    lane_cells = lax.broadcasted_iota(jnp.int32, (cells, LANES), 1)
    parity_cells = (1 - 2 * (lax.broadcasted_iota(jnp.int32, (cells, LANES), 0) & 1)).astype(F32)
    signs = jnp.where(lane_cells >= first_dropped, parity_cells, 1.0)
    row_ids = lax.broadcasted_iota(jnp.int32, (half, LANES), 0)
    low_lanes = lax.broadcasted_iota(jnp.int32, (half, LANES), 1) < LANES // 2
    top_keep = limits[0:1, :]
    bottom_keep = limits[1:2, :]
    top_rows = limits[2:3, :]

    def tile_items(tile):
        if tile < 2:
            return [(4 * tile + k, k) for k in range(4)]
        return [(8, 4), (9, 5)]

    def tile_chunks(tile):
        return [2 * tile, 2 * tile + 1] if tile < 2 else [4]

    for tile in range(3):
        high = jnp.zeros((cells, 2 * LANES), F32)
        low = jnp.zeros((cells, 2 * LANES), F32)
        for item, slot in tile_items(tile):
            item_high, item_low = split(state[item // 2, item % 2] * signs)
            high = high + mm(item_high, place[slot])
            low = low + mm(item_low, place[slot])
        high, low = high.astype(BF16), low.astype(BF16)
        for part in range(2):
            pieces = []
            for side in range(2):
                window = pl.ds(part * rows + side * half, half)
                sums = []
                for which in range(2):
                    lanes = slice(which * LANES, (which + 1) * LANES)
                    table_high, table_low = forward[which, 0, window, :], forward[which, 1, window, :]
                    sums.append(
                        mm(table_high, high[:, lanes])
                        + mm(table_high, low[:, lanes])
                        + mm(table_low, high[:, lanes])
                    )
                pieces.append(jnp.where(row_ids + side * half < top_rows, sums[0], sums[1]))
            if tile < 2:
                own[2 * tile, part] = pieces[0]
                own[2 * tile + 1, part] = pieces[1]
            else:
                own[4, part] = jnp.where(low_lanes, pieces[0], pieces[1])
        for c in tile_chunks(tile):
            @pl.when(is_first)
            def _():
                to_right[c] = own[c]
                rights[c].start()

            @pl.when(is_last)
            def _():
                to_left[c] = own[c]
                lefts[c].start()
        if tile == 0:
            for copy in halos:
                copy.start()

    for f in range(fields):
        outer_own[f] = jnp.where(
            lane_cells < LANES // 2, pltpu.roll(state[f, 1], LANES // 2, 1), state[f, 0]
        )
    for copy in outers:
        copy.start()
    for f in range(fields):
        for x in range(2):
            ext[f, x, pl.ds(RIM, cells), :] = state[f, x]
    for copy in halos:
        copy.wait_recv()

    def turned(ref, c, sign):
        if c < 4:
            window = pl.ds((c % 2) * half, half)
            u, v = turn[0, window, :], turn[1, window, :]
        else:
            u = jnp.where(low_lanes, turn[0, pl.ds(0, half), :], turn[0, pl.ds(half, half), :])
            v = jnp.where(low_lanes, turn[1, pl.ds(0, half), :], turn[1, pl.ds(half, half), :])
        v = v * sign
        cosine, sine = ref[c, 0], ref[c, 1]
        return u * cosine + v * sine, u * sine - v * cosine

    def relay(c):
        @pl.when(jnp.logical_not(is_first))
        def _():
            rights[c].wait_recv()

        @pl.when(jnp.logical_not(is_first) & jnp.logical_not(is_last))
        def _():
            cosine, sine = turned(from_left, c, 1.0)
            to_right[c, 0] = own[c, 0] + cosine
            to_right[c, 1] = own[c, 1] + sine
            rights[c].start()

        @pl.when(jnp.logical_not(is_last))
        def _():
            lefts[c].wait_recv()

        @pl.when(jnp.logical_not(is_first) & jnp.logical_not(is_last))
        def _():
            cosine, sine = turned(from_right, c, -1.0)
            to_left[c, 0] = own[c, 0] + cosine
            to_left[c, 1] = own[c, 1] + sine
            lefts[c].start()

        @pl.when(jnp.logical_not(is_first))
        def _():
            cosine, sine = turned(from_left, c, 1.0)
            own[c, 0] = own[c, 0] + cosine
            own[c, 1] = own[c, 1] + sine

        @pl.when(jnp.logical_not(is_last))
        def _():
            cosine, sine = turned(from_right, c, -1.0)
            own[c, 0] = own[c, 0] + cosine
            own[c, 1] = own[c, 1] + sine

    lane_tall = lax.broadcasted_iota(jnp.int32, (tall, LANES), 1)
    parity_tall = (1 - 2 * (lax.broadcasted_iota(jnp.int32, (tall, LANES), 0) & 1)).astype(F32)

    def restore(tile):
        for side in range(2):
            row = row_ids + side * half
            back_row = rows - 1 - row
            top_weight = jnp.where(row < top_keep, jnp.where(row == 0, 1.0 / NTH, 2.0 / NTH), 0.0)
            bottom_weight = jnp.where(
                back_row < bottom_keep, jnp.where(back_row == 0, 1.0 / NTH, 2.0 / NTH), 0.0
            )
            flips = (1 - 2 * (back_row & 1)).astype(F32)
            if tile == 2:
                mine = low_lanes if side == 0 else jnp.logical_not(low_lanes)
                top_weight = jnp.where(mine, top_weight, 0.0)
                bottom_weight = jnp.where(mine, bottom_weight, 0.0)
            for part in range(2):
                waves = own[2 * tile + side, part] if tile < 2 else own[4, part]
                window = pl.ds(part * rows + side * half, half)
                top_high, top_low = split(waves * top_weight)
                weighted = waves * bottom_weight
                bottom_high, bottom_low = split(weighted)
                far_high, far_low = split(weighted * flips)
                spectrum[0, window, :] = top_high
                spectrum[1, window, :] = top_low
                spectrum[2, window, :] = bottom_high
                spectrum[3, window, :] = bottom_low
                spectrum[4, window, :] = far_high
                spectrum[5, window, :] = far_low

        def series(which, base):
            return (
                mm(inverse[which, 0], spectrum[base])
                + mm(inverse[which, 0], spectrum[base + 1])
                + mm(inverse[which, 1], spectrum[base])
            )

        near = split(jnp.concatenate([series(0, 0), series(1, 2)], axis=1))
        far = split(series(1, 4))
        for item, slot in tile_items(tile):
            f, x = item // 2, item % 2
            filtered = mm(near[0], back[slot]) + mm(near[1], back[slot])
            across = mm(far[0], ghost[slot]) + mm(far[1], ghost[slot])
            raw = ext[f, x]
            cells_now = jnp.where(lane_tall >= first_dropped, raw - parity_tall * filtered, filtered)
            across = -across if f in (2, 3) else across
            ext[f, x] = jnp.where(lane_tall >= LANES - 2, across, cells_now)
            if x == 1:
                centre = pl.ds(RIM, cells)
                inner_own[f] = jnp.where(
                    lane_cells < LANES // 2,
                    ext[f, 0, centre, :],
                    pltpu.roll(ext[f, 1, centre, :], LANES // 2, 1),
                )
                for copy in inners[f]:
                    copy.start()

    relay(0)
    relay(1)
    relay(2)
    restore(0)
    relay(3)
    restore(1)
    relay(4)
    restore(2)

    block = min(32, cells)
    deep = block + 2 * RIM
    lane_deep = lax.broadcasted_iota(jnp.int32, (deep, LANES), 1)
    lane_block = lax.broadcasted_iota(jnp.int32, (block, LANES), 1)
    radius = jnp.where(lane_block >= LANES - 2, lane_block - LANES, lane_block).astype(F32) + 0.5
    inv_radius = 1.0 / radius
    angular = inv_radius * (1.0 / (12.0 * (2.0 * math.pi / NTH)))
    radial = inv_radius * (1.0 / 12.0)

    @pl.loop(0, 2 * (cells // block))
    def _(step):
        x = step % 2
        start = pl.multiple_of((step // 2) * block, block)
        values = [ext[f, x, pl.ds(start, deep), :] for f in range(fields)]
        around, _, _ = fluxes(values, 3)
        centre = [value[RIM : RIM + block] for value in values]
        outward, inverse_density, pressure = fluxes(centre, 2)
        sources = [
            None,
            None,
            (centre[3] * centre[3] * inverse_density + pressure) * inv_radius,
            -(centre[2] * centre[3] * inverse_density) * inv_radius,
            None,
        ]
        for f in range(fields):
            g = around[f]
            turn_term = (
                8.0 * (pltpu.roll(g, deep - 1, 0) - pltpu.roll(g, 1, 0))
                - (pltpu.roll(g, deep - 2, 0) - pltpu.roll(g, 2, 0))
            )[RIM : RIM + block]
            g = outward[f] * radius
            out_term = 8.0 * (pltpu.roll(g, LANES - 1, 1) - pltpu.roll(g, 1, 1)) - (
                pltpu.roll(g, LANES - 2, 1) - pltpu.roll(g, 2, 1)
            )
            total = -(turn_term * angular + out_term * radial)
            if sources[f] is not None:
                total = total + sources[f]
            out[f, x, pl.ds(start, block), :] = (STEP_DT * total)[:, :cycles]

    for copy in outers:
        copy.wait_recv()
    for pair in inners:
        for copy in pair:
            copy.wait_recv()

    low_block = lane_block < LANES // 2

    @pl.loop(0, cells // block)
    def _(step):
        window = pl.ds(pl.multiple_of(step * block, block), block)

        def axial_term(mid, left, right, swapped):
            mids = fluxes([mid[f, window, :] for f in range(fields)], 1)[0]
            lefts_ = fluxes([left[f, window, :] for f in range(fields)], 1)[0]
            rights_ = fluxes([right[f, window, :] for f in range(fields)], 1)[0]
            terms = []
            for f in range(fields):
                back_step, fore_step = mids[f] - lefts_[f], rights_[f] - mids[f]
                if swapped:
                    mixed = jnp.where(low_block, back_step, fore_step)
                else:
                    mixed = jnp.where(low_block, fore_step, back_step)
                terms.append(8.0 * pltpu.roll(mixed, LANES // 2, 1) - (rights_[f] - lefts_[f]))
            return terms

        inner = axial_term(inner_own, inner_left, inner_right, False)
        outer = axial_term(outer_own, outer_left, outer_right, True)
        for f in range(fields):
            first = jnp.where(low_block, inner[f], outer[f])
            second = pltpu.roll(jnp.where(low_block, outer[f], inner[f]), LANES // 2, 1)
            for x, term in ((0, first), (1, second)):
                out[f, x, window, :] = out[f, x, window, :] - (STEP_DT / 12.0) * term[:, :cycles]

    for copy in halos + outers:
        copy.wait_send()
    for pair in inners:
        for copy in pair:
            copy.wait_send()
    for c in range(chunks):
        @pl.when(jnp.logical_not(is_last))
        def _():
            rights[c].wait_send()

        @pl.when(jnp.logical_not(is_first))
        def _():
            lefts[c].wait_send()


def shards(state, start, modes):
    fields, axial, cells, cycles = state.shape
    cfg = plan(cells)
    rows, half = cfg["rows"], cfg["rows"] // 2
    counts = jnp.where(
        np.arange(NIN) < cfg["first_dropped"], modes, NTH // 2 + 1 - modes
    ).astype(jnp.int32)
    limits = jnp.stack(
        [
            jnp.tile(counts[cfg["top"]], cfg["slots"]),
            jnp.tile(counts[cfg["bottom"]], cfg["slots"]),
            jnp.asarray(cfg["top_rows"]),
        ]
    )
    padded = jnp.pad(state, ((0, 0), (0, 0), (0, 0), (0, LANES - cycles)), mode="edge")
    plane = (fields, cells, LANES)
    chunk = (5, 2, half, LANES)
    vmem = pl.BlockSpec(memory_space=pltpu.VMEM)
    step = pl.pallas_call(
        functools.partial(kernel, cfg),
        out_shape=jax.ShapeDtypeStruct(state.shape, F32),
        in_specs=[vmem] * 8,
        out_specs=vmem,
        scratch_shapes=[pltpu.VMEM((fields, axial, cells + 2 * RIM, LANES), F32)]
        + [pltpu.VMEM(plane, F32)] * 6
        + [pltpu.VMEM(chunk, F32)] * 5
        + [pltpu.VMEM((6, 2 * rows, LANES), BF16)]
        + [
            pltpu.SemaphoreType.DMA((2,)),
            pltpu.SemaphoreType.DMA((2,)),
            pltpu.SemaphoreType.DMA((2,)),
            pltpu.SemaphoreType.DMA((2,)),
            pltpu.SemaphoreType.DMA((2, fields)),
            pltpu.SemaphoreType.DMA((2, fields)),
            pltpu.SemaphoreType.DMA((2, 5)),
            pltpu.SemaphoreType.DMA((2, 5)),
        ],
        compiler_params=pltpu.CompilerParams(
            collective_id=0, has_side_effects=True, vmem_limit_bytes=48 * 1024 * 1024
        ),
        name="jet_section",
    )(
        padded,
        limits,
        jnp.asarray(cfg["forward"]),
        jnp.asarray(cfg["inverse"]),
        jnp.asarray(cfg["place"]),
        jnp.asarray(cfg["back"]),
        jnp.asarray(cfg["ghost"]),
        jnp.asarray(cfg["turn"]),
    )
    return start + step


def solution(mesh):
    in_specs = (P(None, "axial", "azim", None), P(None, "axial", "azim", None), P())
    out_specs = P(None, "axial", "azim", None)
    return jax.shard_map(shards, mesh=mesh, in_specs=in_specs, out_specs=out_specs, check_vma=False)
```

```python
import functools
import math

import jax
import jax.numpy as jnp
import numpy as np
from jax import lax
from jax.experimental import pallas as pl
from jax.experimental.pallas import tpu as pltpu
from jax.sharding import PartitionSpec as P

NTH = 1024
NIN = 64
MSTEP = 8
STEP_DT = 0.05
LANES = 128
RIM = 8
F32 = jnp.float32
BF16 = jnp.bfloat16
MESH = pl.DeviceIdType.MESH


def split_np(values):
    high = values.astype(np.float32).astype(jnp.bfloat16)
    low = (values - high.astype(np.float64)).astype(np.float32).astype(jnp.bfloat16)
    return np.stack([high, low])


@functools.lru_cache(None)
def plan(cells):
    order = np.arange(1, NIN + 1)
    kept = np.minimum(2 * MSTEP * order, NTH // 2)
    dropped = NTH // 2 + 1 - np.minimum(MSTEP * order, NTH // 2)
    use_kept = kept <= dropped
    bound = np.where(use_kept, kept, dropped)
    first_dropped = int(np.argmin(use_kept))
    ranked = np.argsort(-bound, kind="stable")
    pairs = NIN // 2
    top, bottom = ranked[:pairs], ranked[::-1][:pairs]
    rows = int(-(-np.max(bound[top] + bound[bottom]) // 32) * 32)
    wave = np.arange(rows)
    angle = lambda n, q: 2 * np.pi * ((n * q) % NTH) / NTH
    forward = []
    for waves in (wave, wave[::-1]):
        phase = angle(np.arange(cells)[None, :], waves[:, None])
        forward.append(split_np(np.concatenate([np.cos(phase), np.sin(phase)], 0)))
    inverse = []
    for waves in (wave, wave[::-1]):
        phase = angle(np.arange(-RIM, cells + RIM)[:, None], waves[None, :])
        inverse.append(split_np(np.concatenate([np.cos(phase), np.sin(phase)], 1)))
    slots = LANES // pairs
    place = np.zeros((slots + slots // 2, LANES, 2 * LANES), np.float32)
    ghost = np.zeros((slots + slots // 2, LANES, LANES), np.float32)
    for slot in range(slots):
        for pair in range(pairs):
            place[slot, top[pair], slot * pairs + pair] = 1
            place[slot, bottom[pair], LANES + slot * pairs + pair] = 1
            if bottom[pair] < 2:
                ghost[slot, slot * pairs + pair, LANES - 1 - bottom[pair]] = 1
    half = slots // 2
    for k in range(half):
        place[slots + k] = place[k] + place[half + k]
        ghost[slots + k] = ghost[k] + ghost[half + k]
    far_rows = int(-(-np.max(bound[:2]) // 16) * 16)
    far_phase = angle(
        np.arange(-RIM, cells + RIM)[:, None] + NTH // 2, np.arange(far_rows)[::-1][None, :]
    )
    far = split_np(np.concatenate([np.cos(far_phase), np.sin(far_phase)], 1))
    groups = (slots + half) // 2
    back = place.transpose(0, 2, 1)
    back = back.reshape(groups, 2, 2 * LANES, LANES).transpose(0, 2, 1, 3)
    ghost = ghost.reshape(groups, 2, LANES, LANES).transpose(0, 2, 1, 3)
    top_rows = np.tile(bound[top], slots)
    wave_of = np.where(wave[:, None] < top_rows[None, :], wave[:, None], rows - 1 - wave[:, None])
    turn = angle(cells, wave_of)
    return dict(
        rows=rows,
        far_rows=far_rows,
        far=far,
        first_dropped=first_dropped,
        top_rows=top_rows.astype(np.int32)[None],
        forward=np.stack(forward),
        inverse=np.stack(inverse),
        place=place.reshape(groups, 2 * LANES, 2 * LANES).astype(jnp.bfloat16),
        back=back.reshape(groups, 2 * LANES, 2 * LANES).astype(jnp.bfloat16),
        ghost=ghost.reshape(groups, LANES, 2 * LANES).astype(jnp.bfloat16),
        turn=np.stack([np.cos(turn), np.sin(turn)]).astype(np.float32),
    )


def split(values):
    high = values.astype(BF16)
    return high, (values - high.astype(F32)).astype(BF16)


def mm(a, b):
    return jnp.dot(a, b, preferred_element_type=F32)


def fluxes(values, direction):
    inverse = 1.0 / values[0]
    velocity = values[direction] * inverse
    kinetic = (values[1] * values[1] + values[2] * values[2] + values[3] * values[3]) * inverse
    pressure = 0.4 * (values[4] - 0.5 * kinetic)
    parts = [
        values[direction],
        values[1] * velocity,
        values[2] * velocity,
        values[3] * velocity,
        (values[4] + pressure) * velocity,
    ]
    parts[direction] = parts[direction] + pressure
    return parts, inverse, pressure


def kernel(
    cfg,
    state, modes, bounds, forward, inverse, place, back, ghost, turn, far_table,
    out,
    ext, rate, outer_own, outer_left, outer_right, inner_own, inner_left, inner_right,
    own, to_right, to_left, from_left, from_right, spectrum,
    halo_send, halo_recv, outer_send, outer_recv, inner_send, inner_recv, wave_send, wave_recv,
):
    rows, first_dropped = cfg["rows"], cfg["first_dropped"]
    half, quarter = rows // 2, rows // 4
    far_rows = cfg["far_rows"]
    fields, cycles, cells = state.shape[0], state.shape[2], state.shape[3]
    tall = cells + 2 * RIM
    d, count = lax.axis_index("azim"), lax.axis_size("azim")
    a, ring = lax.axis_index("axial"), lax.axis_size("axial")
    z_right = {"azim": lax.rem(d + 1, count)}
    z_left = {"azim": lax.rem(d + count - 1, count)}
    x_right = {"axial": lax.rem(a + 1, ring)}
    x_left = {"axial": lax.rem(a + ring - 1, ring)}

    def remote(src, dst, send, recv, device):
        return pltpu.make_async_remote_copy(
            src_ref=src, dst_ref=dst, send_sem=send, recv_sem=recv,
            device_id=device, device_id_type=MESH,
        )

    barrier = pltpu.get_barrier_semaphore()
    for device in (z_right, z_left, x_right, x_left):
        pl.semaphore_signal(barrier, inc=1, device_id=device, device_id_type=MESH)
    for f in range(fields):
        for x in range(2):
            value = state[f, x]
            tail = jnp.broadcast_to(value[cycles - 1 :], (LANES - cycles, cells))
            ext[f, x, pl.ds(RIM, cells), :] = jnp.concatenate([value, tail], axis=0).T
    for f in range(fields):
        low_lane = lax.broadcasted_iota(jnp.int32, (cells, LANES), 1) < LANES // 2
        outer_own[f] = jnp.where(
            low_lane,
            pltpu.roll(ext[f, 1, pl.ds(RIM, cells), :], LANES // 2, 1),
            ext[f, 0, pl.ds(RIM, cells), :],
        )
    pl.semaphore_wait(barrier, 4)

    halos = [
        remote(
            ext.at[:, :, pl.ds(cells, RIM)], ext.at[:, :, pl.ds(0, RIM)],
            halo_send.at[0], halo_recv.at[0], z_right,
        ),
        remote(
            ext.at[:, :, pl.ds(RIM, RIM)], ext.at[:, :, pl.ds(cells + RIM, RIM)],
            halo_send.at[1], halo_recv.at[1], z_left,
        ),
    ]
    outers = [
        remote(outer_own, outer_left, outer_send.at[0], outer_recv.at[0], x_right),
        remote(outer_own, outer_right, outer_send.at[1], outer_recv.at[1], x_left),
    ]
    chunks = 10
    rights = [
        remote(to_right.at[c], from_left.at[c], wave_send.at[0, c], wave_recv.at[0, c], z_right)
        for c in range(chunks)
    ]
    lefts = [
        remote(to_left.at[c], from_right.at[c], wave_send.at[1, c], wave_recv.at[1, c], z_left)
        for c in range(chunks)
    ]
    inners = [
        [
            remote(inner_own.at[f], inner_left.at[f], inner_send.at[0, f], inner_recv.at[0, f], x_right),
            remote(inner_own.at[f], inner_right.at[f], inner_send.at[1, f], inner_recv.at[1, f], x_left),
        ]
        for f in range(fields)
    ]
    is_first, is_last = d == 0, d == count - 1

    lane_cells = lax.broadcasted_iota(jnp.int32, (cells, LANES), 1)
    parity_cells = (1 - 2 * (lax.broadcasted_iota(jnp.int32, (cells, LANES), 0) & 1)).astype(F32)
    signs = jnp.where(lane_cells >= first_dropped, parity_cells, 1.0)
    row_ids = lax.broadcasted_iota(jnp.int32, (quarter, LANES), 0)
    low_lanes = lax.broadcasted_iota(jnp.int32, (quarter, LANES), 1) < LANES // 2
    top_rows = bounds[...]
    cycle_ids = lax.broadcasted_iota(jnp.int32, (8, NIN), 1)
    kept_modes = jnp.broadcast_to(modes[...], (8, NIN))
    counts = split(
        jnp.where(cycle_ids < first_dropped, kept_modes, NTH // 2 + 1 - kept_modes).astype(F32)
    )
    last = place.shape[0] - 1
    keep = sum(
        mm(term, place[last, pl.ds(first, NIN), :]) for term in counts for first in (0, LANES)
    )
    top_keep, bottom_keep = keep[0:1, :LANES], keep[0:1, LANES:]

    def tile_fields(tile):
        if tile < 2:
            return [(2 * tile, 0), (2 * tile + 1, 1)]
        return [(4, 2)]

    def tile_chunks(tile):
        return range(4 * tile, 4 * tile + 4) if tile < 2 else range(8, 10)

    for copy in halos + outers:
        copy.start()
    for tile in range(3):
        high = jnp.zeros((cells, 2 * LANES), F32)
        low = jnp.zeros((cells, 2 * LANES), F32)
        for f, group in tile_fields(tile):
            planes = [ext[f, x, pl.ds(RIM, cells), :] * signs for x in range(2)]
            field_high, field_low = split(jnp.concatenate(planes, axis=1))
            high = high + mm(field_high, place[group])
            low = low + mm(field_low, place[group])
        high, low = high.astype(BF16), low.astype(BF16)
        for part in range(2):
            window = pl.ds(part * rows, rows)
            sums = []
            for which in range(2):
                lanes = slice(which * LANES, (which + 1) * LANES)
                both = mm(
                    forward[which, 0, window, :],
                    jnp.concatenate([high[:, lanes], low[:, lanes]], axis=1),
                )
                sums.append(
                    both[:, :LANES]
                    + both[:, LANES:]
                    + mm(forward[which, 1, window, :], high[:, lanes])
                )
            pieces = []
            for side in range(4):
                part_rows = slice(side * quarter, (side + 1) * quarter)
                pieces.append(
                    jnp.where(
                        row_ids + side * quarter < top_rows, sums[0][part_rows], sums[1][part_rows]
                    )
                )
            for k, c in enumerate(tile_chunks(tile)):
                own[c, part] = pieces[k] if tile < 2 else jnp.where(low_lanes, pieces[k], pieces[k + 2])
        for c in tile_chunks(tile):
            @pl.when(is_first)
            def _():
                to_right[c] = own[c]
                rights[c].start()

            @pl.when(is_last)
            def _():
                to_left[c] = own[c]
                lefts[c].start()

    for copy in halos:
        copy.wait()

    def turned(ref, c, sign):
        if c < 8:
            window = pl.ds((c % 4) * quarter, quarter)
            u, v = turn[0, window, :], turn[1, window, :]
        else:
            low_window = pl.ds((c - 8) * quarter, quarter)
            high_window = pl.ds(half + (c - 8) * quarter, quarter)
            u = jnp.where(low_lanes, turn[0, low_window, :], turn[0, high_window, :])
            v = jnp.where(low_lanes, turn[1, low_window, :], turn[1, high_window, :])
        v = v * sign
        cosine, sine = ref[c, 0], ref[c, 1]
        return u * cosine + v * sine, u * sine - v * cosine

    inside = jnp.logical_not(is_first) & jnp.logical_not(is_last)
    near_first = 2 * d < count

    def pass_right(c, when):
        @pl.when(when & jnp.logical_not(is_first))
        def _():
            rights[c].wait_recv()

        @pl.when(when & inside)
        def _():
            cosine, sine = turned(from_left, c, 1.0)
            to_right[c, 0] = own[c, 0] + cosine
            to_right[c, 1] = own[c, 1] + sine
            rights[c].start()

    def relay(c):
        pass_right(c, near_first)

        @pl.when(jnp.logical_not(is_last))
        def _():
            lefts[c].wait_recv()

        @pl.when(inside)
        def _():
            cosine, sine = turned(from_right, c, -1.0)
            to_left[c, 0] = own[c, 0] + cosine
            to_left[c, 1] = own[c, 1] + sine
            lefts[c].start()

        pass_right(c, jnp.logical_not(near_first))

        @pl.when(jnp.logical_not(is_first))
        def _():
            cosine, sine = turned(from_left, c, 1.0)
            own[c, 0] = own[c, 0] + cosine
            own[c, 1] = own[c, 1] + sine

        @pl.when(jnp.logical_not(is_last))
        def _():
            cosine, sine = turned(from_right, c, -1.0)
            own[c, 0] = own[c, 0] + cosine
            own[c, 1] = own[c, 1] + sine

    lane_tall = lax.broadcasted_iota(jnp.int32, (tall, LANES), 1)
    parity_tall = (1 - 2 * (lax.broadcasted_iota(jnp.int32, (tall, LANES), 0) & 1)).astype(F32)

    def restore(tile):
        for side in range(4):
            row = row_ids + side * quarter
            back_row = rows - 1 - row
            top_weight = jnp.where(
                row.astype(F32) < top_keep, jnp.where(row == 0, 1.0 / NTH, 2.0 / NTH), 0.0
            )
            bottom_weight = jnp.where(
                back_row.astype(F32) < bottom_keep,
                jnp.where(back_row == 0, 1.0 / NTH, 2.0 / NTH),
                0.0,
            )
            if tile == 2:
                mine = low_lanes if side < 2 else jnp.logical_not(low_lanes)
                top_weight = jnp.where(mine, top_weight, 0.0)
                bottom_weight = jnp.where(mine, bottom_weight, 0.0)
            c = 4 * tile + side if tile < 2 else 8 + side % 2
            for part in range(2):
                waves = own[c, part]
                window = pl.ds(part * rows + side * quarter, quarter)
                for which, weight in ((0, top_weight), (1, bottom_weight)):
                    weighted = split(waves * weight)
                    spectrum[which, window, pl.ds(0, LANES)] = weighted[0]
                    spectrum[which, window, pl.ds(LANES, LANES)] = weighted[1]

        def series(which):
            both = mm(inverse[which, 0], spectrum[which])
            return (
                both[:, :LANES]
                + both[:, LANES:]
                + mm(inverse[which, 1], spectrum[which, :, pl.ds(0, LANES)])
            )

        near = split(jnp.concatenate([series(0), series(1)], axis=1))
        waves = jnp.concatenate(
            [spectrum[1, pl.ds((part + 1) * rows - far_rows, far_rows), :] for part in range(2)],
            axis=0,
        )
        both = mm(far_table[0], waves)
        far = split(both[:, :LANES] + both[:, LANES:] + mm(far_table[1], waves[:, :LANES]))
        for f, group in tile_fields(tile):
            filtered = mm(near[0], back[group]) + mm(near[1], back[group])
            across = mm(far[0], ghost[group]) + mm(far[1], ghost[group])
            across = -across if f in (2, 3) else across
            for x in range(2):
                lanes = slice(x * LANES, (x + 1) * LANES)
                raw = ext[f, x]
                now = jnp.where(
                    lane_tall >= first_dropped,
                    raw - parity_tall * filtered[:, lanes],
                    filtered[:, lanes],
                )
                ext[f, x] = jnp.where(lane_tall >= LANES - 2, across[:, lanes], now)
            centre = pl.ds(RIM, cells)
            inner_own[f] = jnp.where(
                lane_cells < LANES // 2,
                ext[f, 0, centre, :],
                pltpu.roll(ext[f, 1, centre, :], LANES // 2, 1),
            )
            for copy in inners[f]:
                copy.start()

    for c in range(5):
        relay(c)
    restore(0)
    for c in range(5, 9):
        relay(c)
    restore(1)
    relay(9)
    restore(2)

    block = min(32, cells)
    deep = block + 2 * RIM
    lane_deep = lax.broadcasted_iota(jnp.int32, (deep, LANES), 1)
    lane_block = lax.broadcasted_iota(jnp.int32, (block, LANES), 1)
    radius = jnp.where(lane_block >= LANES - 2, lane_block - LANES, lane_block).astype(F32) + 0.5
    inv_radius = 1.0 / radius
    angular = inv_radius * (1.0 / (12.0 * (2.0 * math.pi / NTH)))
    radial = inv_radius * (1.0 / 12.0)

    @pl.loop(0, 2 * (cells // block))
    def _(step):
        x = step % 2
        start = pl.multiple_of((step // 2) * block, block)
        values = [ext[f, x, pl.ds(start, deep), :] for f in range(fields)]
        around, _, _ = fluxes(values, 3)
        centre = [value[RIM : RIM + block] for value in values]
        outward, inverse_density, pressure = fluxes(centre, 2)
        sources = [
            None,
            None,
            (centre[3] * centre[3] * inverse_density + pressure) * inv_radius,
            -(centre[2] * centre[3] * inverse_density) * inv_radius,
            None,
        ]
        for f in range(fields):
            g = around[f]
            turn_term = (
                8.0 * (pltpu.roll(g, deep - 1, 0) - pltpu.roll(g, 1, 0))
                - (pltpu.roll(g, deep - 2, 0) - pltpu.roll(g, 2, 0))
            )[RIM : RIM + block]
            g = outward[f] * radius
            out_term = 8.0 * (pltpu.roll(g, LANES - 1, 1) - pltpu.roll(g, 1, 1)) - (
                pltpu.roll(g, LANES - 2, 1) - pltpu.roll(g, 2, 1)
            )
            total = -(turn_term * angular + out_term * radial)
            if sources[f] is not None:
                total = total + sources[f]
            rate[f, x, pl.ds(start, block), :] = STEP_DT * total

    for copy in outers:
        copy.wait_recv()
    for pair in inners:
        for copy in pair:
            copy.wait_recv()

    low_block = lane_block < LANES // 2

    @pl.loop(0, cells // block)
    def _(step):
        window = pl.ds(pl.multiple_of(step * block, block), block)

        def axial_term(mid, left, right, swapped):
            mids = fluxes([mid[f, window, :] for f in range(fields)], 1)[0]
            lefts_ = fluxes([left[f, window, :] for f in range(fields)], 1)[0]
            rights_ = fluxes([right[f, window, :] for f in range(fields)], 1)[0]
            terms = []
            for f in range(fields):
                back_step, fore_step = mids[f] - lefts_[f], rights_[f] - mids[f]
                if swapped:
                    mixed = jnp.where(low_block, back_step, fore_step)
                else:
                    mixed = jnp.where(low_block, fore_step, back_step)
                terms.append(8.0 * pltpu.roll(mixed, LANES // 2, 1) - (rights_[f] - lefts_[f]))
            return terms

        inner = axial_term(inner_own, inner_left, inner_right, False)
        outer = axial_term(outer_own, outer_left, outer_right, True)
        for f in range(fields):
            first = jnp.where(low_block, inner[f], outer[f])
            second = pltpu.roll(jnp.where(low_block, outer[f], inner[f]), LANES // 2, 1)
            for x, term in ((0, first), (1, second)):
                rate[f, x, window, :] = rate[f, x, window, :] - (STEP_DT / 12.0) * term

    for f in range(fields):
        for x in range(2):
            out[f, x] = rate[f, x].T[:cycles]

    for copy in outers:
        copy.wait_send()
    for pair in inners:
        for copy in pair:
            copy.wait_send()
    for c in range(chunks):
        @pl.when(jnp.logical_not(is_last))
        def _():
            rights[c].wait_send()

        @pl.when(jnp.logical_not(is_first))
        def _():
            lefts[c].wait_send()


def shards(state, start, modes):
    fields, axial, cells, cycles = state.shape
    cfg = plan(cells)
    rows = cfg["rows"]
    turned = state.transpose(0, 1, 3, 2)
    plane = (fields, cells, LANES)
    chunk = (10, 2, rows // 4, LANES)
    vmem = pl.BlockSpec(memory_space=pltpu.VMEM)
    step = pl.pallas_call(
        functools.partial(kernel, cfg),
        out_shape=jax.ShapeDtypeStruct(turned.shape, F32),
        in_specs=[vmem] * 10,
        out_specs=vmem,
        scratch_shapes=[pltpu.VMEM((fields, axial, cells + 2 * RIM, LANES), F32)]
        + [pltpu.VMEM((fields, axial, cells, LANES), F32)]
        + [pltpu.VMEM(plane, F32)] * 6
        + [pltpu.VMEM(chunk, F32)] * 5
        + [pltpu.VMEM((2, 2 * rows, 2 * LANES), BF16)]
        + [
            pltpu.SemaphoreType.DMA((2,)),
            pltpu.SemaphoreType.DMA((2,)),
            pltpu.SemaphoreType.DMA((2,)),
            pltpu.SemaphoreType.DMA((2,)),
            pltpu.SemaphoreType.DMA((2, fields)),
            pltpu.SemaphoreType.DMA((2, fields)),
            pltpu.SemaphoreType.DMA((2, 10)),
            pltpu.SemaphoreType.DMA((2, 10)),
        ],
        compiler_params=pltpu.CompilerParams(
            collective_id=0, has_side_effects=True, vmem_limit_bytes=48 * 1024 * 1024
        ),
        name="jet_section",
    )(
        turned,
        modes.reshape(1, NIN),
        jnp.asarray(cfg["top_rows"]),
        jnp.asarray(cfg["forward"]),
        jnp.asarray(cfg["inverse"]),
        jnp.asarray(cfg["place"]),
        jnp.asarray(cfg["back"]),
        jnp.asarray(cfg["ghost"]),
        jnp.asarray(cfg["turn"]),
        jnp.asarray(cfg["far"]),
    )
    return start + step.transpose(0, 1, 3, 2)


def solution(mesh):
    in_specs = (P(None, "axial", "azim", None), P(None, "axial", "azim", None), P())
    out_specs = P(None, "axial", "azim", None)
    return jax.shard_map(shards, mesh=mesh, in_specs=in_specs, out_specs=out_specs, check_vma=False)
```

```python
import functools
import math

import jax
import jax.numpy as jnp
import numpy as np
from jax import lax
from jax.experimental import pallas as pl
from jax.experimental.pallas import tpu as pltpu
from jax.sharding import PartitionSpec as P

NTH = 1024
NIN = 64
MSTEP = 8
STEP_DT = 0.05
LANES = 128
RIM = 8
F32 = jnp.float32
BF16 = jnp.bfloat16
MESH = pl.DeviceIdType.MESH


def split_np(values):
    high = values.astype(np.float32).astype(jnp.bfloat16)
    low = (values - high.astype(np.float64)).astype(np.float32).astype(jnp.bfloat16)
    return np.stack([high, low])


@functools.lru_cache(None)
def plan(cells):
    order = np.arange(1, NIN + 1)
    kept = np.minimum(2 * MSTEP * order, NTH // 2)
    dropped = NTH // 2 + 1 - np.minimum(MSTEP * order, NTH // 2)
    use_kept = kept <= dropped
    bound = np.where(use_kept, kept, dropped)
    first_dropped = int(np.argmin(use_kept))
    ranked = np.argsort(-bound, kind="stable")
    pairs = NIN // 2
    top, bottom = ranked[:pairs], ranked[::-1][:pairs]
    rows = int(-(-np.max(bound[top] + bound[bottom]) // 32) * 32)
    wave = np.arange(rows)
    angle = lambda n, q: 2 * np.pi * ((n * q) % NTH) / NTH
    forward = []
    for waves in (wave, wave[::-1]):
        phase = angle(np.arange(cells)[None, :], waves[:, None])
        forward.append(split_np(np.concatenate([np.cos(phase), np.sin(phase)], 0)))
    inverse = []
    for waves in (wave, wave[::-1]):
        phase = angle(np.arange(-RIM, cells + RIM)[:, None], waves[None, :])
        inverse.append(split_np(np.concatenate([np.cos(phase), np.sin(phase)], 1)))
    slots = LANES // pairs
    place = np.zeros((slots + slots // 2, LANES, 2 * LANES), np.float32)
    ghost = np.zeros((slots + slots // 2, LANES, LANES), np.float32)
    for slot in range(slots):
        for pair in range(pairs):
            place[slot, top[pair], slot * pairs + pair] = 1
            place[slot, bottom[pair], LANES + slot * pairs + pair] = 1
            if bottom[pair] < 2:
                ghost[slot, slot * pairs + pair, LANES - 1 - bottom[pair]] = 1
    half = slots // 2
    for k in range(half):
        place[slots + k] = place[k] + place[half + k]
        ghost[slots + k] = ghost[k] + ghost[half + k]
    far_rows = int(-(-np.max(bound[:2]) // 16) * 16)
    far_phase = angle(
        np.arange(-RIM, cells + RIM)[:, None] + NTH // 2, np.arange(far_rows)[::-1][None, :]
    )
    far = split_np(np.concatenate([np.cos(far_phase), np.sin(far_phase)], 1))
    groups = (slots + half) // 2
    back = place.transpose(0, 2, 1)
    back = back.reshape(groups, 2, 2 * LANES, LANES).transpose(0, 2, 1, 3)
    ghost = ghost.reshape(groups, 2, LANES, LANES).transpose(0, 2, 1, 3)
    top_rows = np.tile(bound[top], slots)
    wave_of = np.where(wave[:, None] < top_rows[None, :], wave[:, None], rows - 1 - wave[:, None])
    turn = angle(cells, wave_of)
    return dict(
        rows=rows,
        far_rows=far_rows,
        far=far,
        first_dropped=first_dropped,
        top_rows=top_rows.astype(np.int32)[None],
        forward=np.stack(forward),
        inverse=np.stack(inverse),
        place=place.reshape(groups, 2 * LANES, 2 * LANES).astype(jnp.bfloat16),
        back=back.reshape(groups, 2 * LANES, 2 * LANES).astype(jnp.bfloat16),
        ghost=ghost.reshape(groups, LANES, 2 * LANES).astype(jnp.bfloat16),
        turn=np.stack([np.cos(turn), np.sin(turn)]).astype(np.float32),
    )


def split(values):
    high = values.astype(BF16)
    return high, (values - high.astype(F32)).astype(BF16)


def mm(a, b):
    return jnp.dot(a, b, preferred_element_type=F32)


def fluxes(values, direction):
    inverse = 1.0 / values[0]
    velocity = values[direction] * inverse
    kinetic = (values[1] * values[1] + values[2] * values[2] + values[3] * values[3]) * inverse
    pressure = 0.4 * (values[4] - 0.5 * kinetic)
    parts = [
        values[direction],
        values[1] * velocity,
        values[2] * velocity,
        values[3] * velocity,
        (values[4] + pressure) * velocity,
    ]
    parts[direction] = parts[direction] + pressure
    return parts, inverse, pressure


def kernel(
    cfg,
    state, modes, bounds, *refs,
):
    stored, out, refs = refs[:7], refs[7], refs[8:]
    loaded, table_sem, refs = refs[:7], refs[7], refs[8:]
    forward, inverse, place, back, ghost, turn, far_table = loaded
    (
        ext, rate, outer_own, outer_left, outer_right, inner_own, inner_left, inner_right,
        own, to_right, to_left, from_left, from_right, spectrum,
        halo_send, halo_recv, outer_send, outer_recv, inner_send, inner_recv, wave_send, wave_recv,
    ) = refs
    tables = [
        pltpu.make_async_copy(stored[k], loaded[k], table_sem.at[k]) for k in range(len(stored))
    ]
    for k in (2, 0, 5, 1, 3, 4, 6):
        tables[k].start()
    rows, first_dropped = cfg["rows"], cfg["first_dropped"]
    half, quarter = rows // 2, rows // 4
    far_rows = cfg["far_rows"]
    fields, cycles, cells = state.shape[0], state.shape[2], state.shape[3]
    tall = cells + 2 * RIM
    d, count = lax.axis_index("azim"), lax.axis_size("azim")
    a, ring = lax.axis_index("axial"), lax.axis_size("axial")
    z_right = {"azim": lax.rem(d + 1, count)}
    z_left = {"azim": lax.rem(d + count - 1, count)}
    x_right = {"axial": lax.rem(a + 1, ring)}
    x_left = {"axial": lax.rem(a + ring - 1, ring)}

    def remote(src, dst, send, recv, device):
        return pltpu.make_async_remote_copy(
            src_ref=src, dst_ref=dst, send_sem=send, recv_sem=recv,
            device_id=device, device_id_type=MESH,
        )

    barrier = pltpu.get_barrier_semaphore()
    for device in (z_right, z_left, x_right, x_left):
        pl.semaphore_signal(barrier, inc=1, device_id=device, device_id_type=MESH)
    for f in range(fields):
        for x in range(2):
            value = state[f, x]
            tail = jnp.broadcast_to(value[cycles - 1 :], (LANES - cycles, cells))
            ext[f, x, pl.ds(RIM, cells), :] = jnp.concatenate([value, tail], axis=0).T
    for f in range(fields):
        low_lane = lax.broadcasted_iota(jnp.int32, (cells, LANES), 1) < LANES // 2
        outer_own[f] = jnp.where(
            low_lane,
            pltpu.roll(ext[f, 1, pl.ds(RIM, cells), :], LANES // 2, 1),
            ext[f, 0, pl.ds(RIM, cells), :],
        )
    pl.semaphore_wait(barrier, 4)

    halos = [
        remote(
            ext.at[:, :, pl.ds(cells, RIM)], ext.at[:, :, pl.ds(0, RIM)],
            halo_send.at[0], halo_recv.at[0], z_right,
        ),
        remote(
            ext.at[:, :, pl.ds(RIM, RIM)], ext.at[:, :, pl.ds(cells + RIM, RIM)],
            halo_send.at[1], halo_recv.at[1], z_left,
        ),
    ]
    outers = [
        remote(outer_own, outer_left, outer_send.at[0], outer_recv.at[0], x_right),
        remote(outer_own, outer_right, outer_send.at[1], outer_recv.at[1], x_left),
    ]
    chunks = 10
    rights = [
        remote(to_right.at[c], from_left.at[c], wave_send.at[0, c], wave_recv.at[0, c], z_right)
        for c in range(chunks)
    ]
    lefts = [
        remote(to_left.at[c], from_right.at[c], wave_send.at[1, c], wave_recv.at[1, c], z_left)
        for c in range(chunks)
    ]
    inners = [
        [
            remote(inner_own.at[f], inner_left.at[f], inner_send.at[0, f], inner_recv.at[0, f], x_right),
            remote(inner_own.at[f], inner_right.at[f], inner_send.at[1, f], inner_recv.at[1, f], x_left),
        ]
        for f in range(fields)
    ]
    is_first, is_last = d == 0, d == count - 1

    lane_cells = lax.broadcasted_iota(jnp.int32, (cells, LANES), 1)
    parity_cells = (1 - 2 * (lax.broadcasted_iota(jnp.int32, (cells, LANES), 0) & 1)).astype(F32)
    signs = jnp.where(lane_cells >= first_dropped, parity_cells, 1.0)
    row_ids = lax.broadcasted_iota(jnp.int32, (quarter, LANES), 0)
    low_lanes = lax.broadcasted_iota(jnp.int32, (quarter, LANES), 1) < LANES // 2
    tables[2].wait()
    top_rows = bounds[...]
    cycle_ids = lax.broadcasted_iota(jnp.int32, (8, NIN), 1)
    kept_modes = jnp.broadcast_to(modes[...], (8, NIN))
    counts = split(
        jnp.where(cycle_ids < first_dropped, kept_modes, NTH // 2 + 1 - kept_modes).astype(F32)
    )
    last = place.shape[0] - 1
    keep = sum(
        mm(term, place[last, pl.ds(first, NIN), :]) for term in counts for first in (0, LANES)
    )
    top_keep, bottom_keep = keep[0:1, :LANES], keep[0:1, LANES:]

    def tile_fields(tile):
        if tile < 2:
            return [(2 * tile, 0), (2 * tile + 1, 1)]
        return [(4, 2)]

    def tile_chunks(tile):
        return range(4 * tile, 4 * tile + 4) if tile < 2 else range(8, 10)

    for copy in halos + outers:
        copy.start()
    tables[0].wait()
    for tile in range(3):
        high = jnp.zeros((cells, 2 * LANES), F32)
        low = jnp.zeros((cells, 2 * LANES), F32)
        for f, group in tile_fields(tile):
            planes = [ext[f, x, pl.ds(RIM, cells), :] * signs for x in range(2)]
            field_high, field_low = split(jnp.concatenate(planes, axis=1))
            high = high + mm(field_high, place[group])
            low = low + mm(field_low, place[group])
        high, low = high.astype(BF16), low.astype(BF16)
        for part in range(2):
            window = pl.ds(part * rows, rows)
            sums = []
            for which in range(2):
                lanes = slice(which * LANES, (which + 1) * LANES)
                both = mm(
                    forward[which, 0, window, :],
                    jnp.concatenate([high[:, lanes], low[:, lanes]], axis=1),
                )
                sums.append(
                    both[:, :LANES]
                    + both[:, LANES:]
                    + mm(forward[which, 1, window, :], high[:, lanes])
                )
            pieces = []
            for side in range(4):
                part_rows = slice(side * quarter, (side + 1) * quarter)
                pieces.append(
                    jnp.where(
                        row_ids + side * quarter < top_rows, sums[0][part_rows], sums[1][part_rows]
                    )
                )
            for k, c in enumerate(tile_chunks(tile)):
                own[c, part] = pieces[k] if tile < 2 else jnp.where(low_lanes, pieces[k], pieces[k + 2])
        for c in tile_chunks(tile):
            @pl.when(is_first)
            def _():
                to_right[c] = own[c]
                rights[c].start()

            @pl.when(is_last)
            def _():
                to_left[c] = own[c]
                lefts[c].start()

    for copy in halos:
        copy.wait()
    for k in (5, 1, 3, 4, 6):
        tables[k].wait()

    def turned(ref, c, sign):
        if c < 8:
            window = pl.ds((c % 4) * quarter, quarter)
            u, v = turn[0, window, :], turn[1, window, :]
        else:
            low_window = pl.ds((c - 8) * quarter, quarter)
            high_window = pl.ds(half + (c - 8) * quarter, quarter)
            u = jnp.where(low_lanes, turn[0, low_window, :], turn[0, high_window, :])
            v = jnp.where(low_lanes, turn[1, low_window, :], turn[1, high_window, :])
        v = v * sign
        cosine, sine = ref[c, 0], ref[c, 1]
        return u * cosine + v * sine, u * sine - v * cosine

    inside = jnp.logical_not(is_first) & jnp.logical_not(is_last)
    near_first = 2 * d < count

    def pass_right(c, when):
        @pl.when(when & jnp.logical_not(is_first))
        def _():
            rights[c].wait_recv()

        @pl.when(when & inside)
        def _():
            cosine, sine = turned(from_left, c, 1.0)
            to_right[c, 0] = own[c, 0] + cosine
            to_right[c, 1] = own[c, 1] + sine
            rights[c].start()

    def pass_left(c, when):
        @pl.when(when & jnp.logical_not(is_last))
        def _():
            lefts[c].wait_recv()

        @pl.when(when & inside)
        def _():
            cosine, sine = turned(from_right, c, -1.0)
            to_left[c, 0] = own[c, 0] + cosine
            to_left[c, 1] = own[c, 1] + sine
            lefts[c].start()

    def relay_near(c):
        pass_right(c, near_first)
        pass_left(c, jnp.logical_not(near_first))

    def relay_far(c):
        pass_left(c, near_first)
        pass_right(c, jnp.logical_not(near_first))

        @pl.when(jnp.logical_not(is_first))
        def _():
            cosine, sine = turned(from_left, c, 1.0)
            own[c, 0] = own[c, 0] + cosine
            own[c, 1] = own[c, 1] + sine

        @pl.when(jnp.logical_not(is_last))
        def _():
            cosine, sine = turned(from_right, c, -1.0)
            own[c, 0] = own[c, 0] + cosine
            own[c, 1] = own[c, 1] + sine

    lane_tall = lax.broadcasted_iota(jnp.int32, (tall, LANES), 1)
    parity_tall = (1 - 2 * (lax.broadcasted_iota(jnp.int32, (tall, LANES), 0) & 1)).astype(F32)

    def restore(tile):
        for side in range(4):
            row = row_ids + side * quarter
            back_row = rows - 1 - row
            top_weight = jnp.where(
                row.astype(F32) < top_keep, jnp.where(row == 0, 1.0 / NTH, 2.0 / NTH), 0.0
            )
            bottom_weight = jnp.where(
                back_row.astype(F32) < bottom_keep,
                jnp.where(back_row == 0, 1.0 / NTH, 2.0 / NTH),
                0.0,
            )
            if tile == 2:
                mine = low_lanes if side < 2 else jnp.logical_not(low_lanes)
                top_weight = jnp.where(mine, top_weight, 0.0)
                bottom_weight = jnp.where(mine, bottom_weight, 0.0)
            c = 4 * tile + side if tile < 2 else 8 + side % 2
            for part in range(2):
                waves = own[c, part]
                window = pl.ds(part * rows + side * quarter, quarter)
                for which, weight in ((0, top_weight), (1, bottom_weight)):
                    weighted = split(waves * weight)
                    spectrum[which, window, pl.ds(0, LANES)] = weighted[0]
                    spectrum[which, window, pl.ds(LANES, LANES)] = weighted[1]

        def series(which):
            both = mm(inverse[which, 0], spectrum[which])
            return (
                both[:, :LANES]
                + both[:, LANES:]
                + mm(inverse[which, 1], spectrum[which, :, pl.ds(0, LANES)])
            )

        near = split(jnp.concatenate([series(0), series(1)], axis=1))
        waves = jnp.concatenate(
            [spectrum[1, pl.ds((part + 1) * rows - far_rows, far_rows), :] for part in range(2)],
            axis=0,
        )
        both = mm(far_table[0], waves)
        far = split(both[:, :LANES] + both[:, LANES:] + mm(far_table[1], waves[:, :LANES]))
        for f, group in tile_fields(tile):
            filtered = mm(near[0], back[group]) + mm(near[1], back[group])
            across = mm(far[0], ghost[group]) + mm(far[1], ghost[group])
            across = -across if f in (2, 3) else across
            for x in range(2):
                lanes = slice(x * LANES, (x + 1) * LANES)
                raw = ext[f, x]
                now = jnp.where(
                    lane_tall >= first_dropped,
                    raw - parity_tall * filtered[:, lanes],
                    filtered[:, lanes],
                )
                ext[f, x] = jnp.where(lane_tall >= LANES - 2, across[:, lanes], now)
            centre = pl.ds(RIM, cells)
            inner_own[f] = jnp.where(
                lane_cells < LANES // 2,
                ext[f, 0, centre, :],
                pltpu.roll(ext[f, 1, centre, :], LANES // 2, 1),
            )
            for copy in inners[f]:
                copy.start()

    lag = 3
    for step in range(chunks + lag):
        if step < chunks:
            relay_near(step)
        c = step - lag
        if c >= 0:
            relay_far(c)
            if c in (3, 7, 9):
                restore(c // 4)

    block = min(32, cells)
    deep = block + 2 * RIM
    lane_deep = lax.broadcasted_iota(jnp.int32, (deep, LANES), 1)
    lane_block = lax.broadcasted_iota(jnp.int32, (block, LANES), 1)
    radius = jnp.where(lane_block >= LANES - 2, lane_block - LANES, lane_block).astype(F32) + 0.5
    inv_radius = 1.0 / radius
    angular = inv_radius * (1.0 / (12.0 * (2.0 * math.pi / NTH)))
    radial = inv_radius * (1.0 / 12.0)

    @pl.loop(0, 2 * (cells // block))
    def _(step):
        x = step % 2
        start = pl.multiple_of((step // 2) * block, block)
        values = [ext[f, x, pl.ds(start, deep), :] for f in range(fields)]
        around, _, _ = fluxes(values, 3)
        centre = [value[RIM : RIM + block] for value in values]
        outward, inverse_density, pressure = fluxes(centre, 2)
        sources = [
            None,
            None,
            (centre[3] * centre[3] * inverse_density + pressure) * inv_radius,
            -(centre[2] * centre[3] * inverse_density) * inv_radius,
            None,
        ]
        for f in range(fields):
            g = around[f]
            turn_term = (
                8.0 * (pltpu.roll(g, deep - 1, 0) - pltpu.roll(g, 1, 0))
                - (pltpu.roll(g, deep - 2, 0) - pltpu.roll(g, 2, 0))
            )[RIM : RIM + block]
            g = outward[f] * radius
            out_term = 8.0 * (pltpu.roll(g, LANES - 1, 1) - pltpu.roll(g, 1, 1)) - (
                pltpu.roll(g, LANES - 2, 1) - pltpu.roll(g, 2, 1)
            )
            total = -(turn_term * angular + out_term * radial)
            if sources[f] is not None:
                total = total + sources[f]
            rate[f, x, pl.ds(start, block), :] = STEP_DT * total

    for copy in outers:
        copy.wait_recv()
    for pair in inners:
        for copy in pair:
            copy.wait_recv()

    low_block = lane_block < LANES // 2

    @pl.loop(0, cells // block)
    def _(step):
        window = pl.ds(pl.multiple_of(step * block, block), block)

        def axial_term(mid, left, right, swapped):
            mids = fluxes([mid[f, window, :] for f in range(fields)], 1)[0]
            lefts_ = fluxes([left[f, window, :] for f in range(fields)], 1)[0]
            rights_ = fluxes([right[f, window, :] for f in range(fields)], 1)[0]
            terms = []
            for f in range(fields):
                back_step, fore_step = mids[f] - lefts_[f], rights_[f] - mids[f]
                if swapped:
                    mixed = jnp.where(low_block, back_step, fore_step)
                else:
                    mixed = jnp.where(low_block, fore_step, back_step)
                terms.append(8.0 * pltpu.roll(mixed, LANES // 2, 1) - (rights_[f] - lefts_[f]))
            return terms

        inner = axial_term(inner_own, inner_left, inner_right, False)
        outer = axial_term(outer_own, outer_left, outer_right, True)
        for f in range(fields):
            first = jnp.where(low_block, inner[f], outer[f])
            second = pltpu.roll(jnp.where(low_block, outer[f], inner[f]), LANES // 2, 1)
            for x, term in ((0, first), (1, second)):
                rate[f, x, window, :] = rate[f, x, window, :] - (STEP_DT / 12.0) * term

    for f in range(fields):
        for x in range(2):
            out[f, x] = rate[f, x].T[:cycles]

    for copy in outers:
        copy.wait_send()
    for pair in inners:
        for copy in pair:
            copy.wait_send()
    for c in range(chunks):
        @pl.when(jnp.logical_not(is_last))
        def _():
            rights[c].wait_send()

        @pl.when(jnp.logical_not(is_first))
        def _():
            lefts[c].wait_send()


def shards(state, start, modes):
    fields, axial, cells, cycles = state.shape
    cfg = plan(cells)
    rows = cfg["rows"]
    turned = state.transpose(0, 1, 3, 2)
    plane = (fields, cells, LANES)
    chunk = (10, 2, rows // 4, LANES)
    names = ("forward", "inverse", "place", "back", "ghost", "turn", "far")
    tables = [jnp.asarray(cfg[name]) for name in names]
    vmem = pl.BlockSpec(memory_space=pltpu.VMEM)
    step = pl.pallas_call(
        functools.partial(kernel, cfg),
        out_shape=jax.ShapeDtypeStruct(turned.shape, F32),
        in_specs=[vmem] * 3 + [pl.BlockSpec(memory_space=pltpu.HBM)] * 7,
        out_specs=vmem,
        scratch_shapes=[pltpu.VMEM(table.shape, table.dtype) for table in tables]
        + [pltpu.SemaphoreType.DMA((7,))]
        + [pltpu.VMEM((fields, axial, cells + 2 * RIM, LANES), F32)]
        + [pltpu.VMEM((fields, axial, cells, LANES), F32)]
        + [pltpu.VMEM(plane, F32)] * 6
        + [pltpu.VMEM(chunk, F32)] * 5
        + [pltpu.VMEM((2, 2 * rows, 2 * LANES), BF16)]
        + [
            pltpu.SemaphoreType.DMA((2,)),
            pltpu.SemaphoreType.DMA((2,)),
            pltpu.SemaphoreType.DMA((2,)),
            pltpu.SemaphoreType.DMA((2,)),
            pltpu.SemaphoreType.DMA((2, fields)),
            pltpu.SemaphoreType.DMA((2, fields)),
            pltpu.SemaphoreType.DMA((2, 10)),
            pltpu.SemaphoreType.DMA((2, 10)),
        ],
        compiler_params=pltpu.CompilerParams(
            collective_id=0, has_side_effects=True, vmem_limit_bytes=48 * 1024 * 1024
        ),
        name="jet_section",
    )(
        turned,
        modes.reshape(1, NIN),
        jnp.asarray(cfg["top_rows"]),
        *tables,
    )
    return start + step.transpose(0, 1, 3, 2)


def solution(mesh):
    in_specs = (P(None, "axial", "azim", None), P(None, "axial", "azim", None), P())
    out_specs = P(None, "axial", "azim", None)
    return jax.shard_map(shards, mesh=mesh, in_specs=in_specs, out_specs=out_specs, check_vma=False)
```
